512 devices in a mesh: gx: 4 (over x), gy: 16 (over z, core), gz: 8 (over y).
Axes of the slice: x: 4, y: 8, z: 8, core: 2. Of those that a mesh axis runs over, the one named last changes fastest.
Arguments:
- right_side: float32 [64, 128, 1024], P('gx', 'gy', 'gz'), may hold values from -24 to 24
- conduct: float32 [64, 128, 1024], P('gx', 'gy', 'gz'), may hold values from 0.3 to 3
- mass: float32 [64, 128, 1024], P('gx', 'gy', 'gz'), may hold values from 0.01 to 0.2
- aggregate_of: int32 [16, 32, 256], P('gx', 'gy', 'gz'), may hold values from 0 to 2047
- coarse_inverse: float32 [2048, 2048], P('gy'), as said below
Outputs:
- solution_field: float32 [64, 128, 1024], P('gx', 'gy', 'gz')
The draws below stay inside these ranges and needn't reach their ends.
Inputs may be any that keep to these rules, and one draw needn't show every extreme that they name: coarse_inverse is symmetric.
All inputs are finite; a program needn't handle non-finite values.
Results may differ from the reference program's by a relative error of at most 0.00015.
Values sent between devices are 32-bit elements; how exact they have to be, the bound alone decides.
A program may use at most 64 MiB of HBM per device.

```python
import math
import jax
import jax.numpy as jnp
from jax import lax

LEVELS = 3
CYCLES = 2
NX = 64
NY = 128
NZ = 1024
NAGG = 2048


def draw_coarse_inverse(key, part):
    first_key, second_key = jax.random.split(jax.random.fold_in(key, 17))
    base = jax.random.normal(first_key, (NAGG, NAGG), jnp.float32)
    symmetric = (base + base.T) * 0.5
    diagonal = jax.random.uniform(second_key, (NAGG,), jnp.float32, 0.5, 1.5)
    per_aggregate = NX // 2 ** (LEVELS - 1) * (NY // 2 ** (LEVELS - 1)) * (NZ // 2 ** (LEVELS - 1)) / NAGG
    factor = 1.0 / (8.0 * per_aggregate)
    matrix = jnp.diag(diagonal) + symmetric * (1.0 / jnp.sqrt(jnp.float32(NAGG)))
    return (factor * matrix).astype(jnp.float32)


def plant(result, key, smallest, high):
    extent = result.shape
    place = [jax.random.randint(jax.random.fold_in(key, axis), (), 0, extent[axis]) for axis in range(len(extent))]
    result = result.at[tuple(place)].set(smallest)
    longest = extent.index(max(extent))
    place[longest] = (place[longest] + 1) % extent[longest]
    return result.at[tuple(place)].set(high)


def steps_of(rng, shape, cuts, smallest, largest):
    loudness = 1.0
    for axis_at, shards_of in cuts:
        steps = jax.random.uniform(jax.random.fold_in(jax.random.fold_in(rng, 6), axis_at), (shards_of,), jnp.float32, smallest / len(cuts), largest / len(cuts))
        loudness = loudness * jnp.repeat(jnp.exp(steps), shape[axis_at] // shards_of).reshape((-1,) + (1,) * (len(shape) - 1 - axis_at))
    return loudness


def noise(own_key, extent, scale, limit, shards=(), dtype=jnp.bfloat16):
    values = jax.random.normal(own_key, extent, jnp.float32) * scale
    if len(shards) > 0:
        values = steps_of(own_key, extent, shards, -0.22, 0.18) * values
    return jnp.clip(values, min=-limit, max=limit).astype(dtype)


def setup_inputs(seed: int = 0) -> dict:
    key_list = jax.random.split(jax.random.key(seed), 6)
    right_side = noise(key_list[0], (NX, NY, NZ), 4.0, 24.0, ((0, 4), (1, 16), (2, 8)), jnp.float32)
    conduct = jnp.clip(jnp.exp(math.log(3.0) - 2.3025851 * jax.random.uniform(key_list[1], (NX, NY, NZ), jnp.float32) ** steps_of(key_list[1], (NX, NY, NZ), ((0, 4), (1, 16), (2, 8)), -0.2, 0.2)), 0.3, 3.0)
    mass = jnp.clip(jnp.exp(math.log(0.2) - 2.9957323 * jax.random.uniform(key_list[2], (NX, NY, NZ), jnp.float32) ** steps_of(key_list[2], (NX, NY, NZ), ((0, 4), (1, 16), (2, 8)), -0.2, 0.2)), 0.01, 0.2)
    aggregate_of = plant(jax.random.randint(key_list[3], (NX // 2**(LEVELS - 1), NY // 2**(LEVELS - 1), NZ // 2**(LEVELS - 1)), 0, NAGG), jax.random.fold_in(key_list[3], 1), 0, NAGG - 1).astype(jnp.int32)
    coarse_inverse = draw_coarse_inverse(jax.random.fold_in(key_list[5], 71), 0)
    return dict(right_side=right_side, conduct=conduct, mass=mass, aggregate_of=aggregate_of, coarse_inverse=coarse_inverse)


stencil_offsets = [(first, second, third) for first in (-1, 0, 1) for second in (-1, 0, 1) for third in (-1, 0, 1) if (first, second, third) != (0, 0, 0)]
stencil_weights = (0.0, 1.0, 0.5, 0.25)
OMEGA = 0.7


def shifted_sum(padded):
    shape = tuple(n - 2 for n in padded.shape)
    total = jnp.zeros(shape, jnp.float32)
    for offset in stencil_offsets:
        weight = stencil_weights[abs(offset[0]) + abs(offset[1]) + abs(offset[2])]
        piece = padded[1 + offset[0]:1 + offset[0] + shape[0], 1 + offset[1]:1 + offset[1] + shape[1], 1 + offset[2]:1 + offset[2] + shape[2]]
        total = total + weight * piece
    return total


def pool_sum(field):
    shape = field.shape
    return field.reshape(shape[0] // 2, 2, shape[1] // 2, 2, shape[2] // 2, 2).sum(axis=(1, 3, 5))


def spread_up(field):
    return jnp.repeat(jnp.repeat(jnp.repeat(field, 2, axis=0), 2, axis=1), 2, axis=2)


def apply_operator(field, level_data):
    padded_k, scaled_k, diagonal = level_data
    padded_v = jnp.pad(field, 1)
    return diagonal * field - scaled_k * shifted_sum(padded_k * padded_v)


def sweep(field, source, level_data):
    diagonal = level_data[2]
    if field is None:
        return OMEGA * source / diagonal
    return field + OMEGA * (source - apply_operator(field, level_data)) / diagonal


def reference(right_side, conduct, mass, aggregate_of, coarse_inverse):
    data = []
    conduct_lv = conduct
    mass_lv = mass
    for level in range(LEVELS):
        padded_k = jnp.pad(conduct_lv - 1.0, 1) + 1.0
        scaled_k = (2.0 ** level) * conduct_lv
        diagonal = scaled_k * shifted_sum(padded_k) + mass_lv
        data.append((padded_k, scaled_k, diagonal))
        if level + 1 < LEVELS:
            conduct_lv = pool_sum(conduct_lv) * 0.125
            mass_lv = pool_sum(mass_lv)

    def aggregate_fix(residual):
        sums = jax.ops.segment_sum(residual.reshape(-1), aggregate_of.reshape(-1), num_segments=NAGG)
        correction = jnp.dot(coarse_inverse, sums, precision=lax.Precision.HIGHEST)
        return correction[aggregate_of]

    def cycle(level, source, field):
        field = sweep(field, source, data[level])
        field = sweep(field, source, data[level])
        residual = source - apply_operator(field, data[level])
        if level + 1 < LEVELS:
            field = field + spread_up(cycle(level + 1, pool_sum(residual), None))
        else:
            field = field + aggregate_fix(residual)
        field = sweep(field, source, data[level])
        field = sweep(field, source, data[level])
        return field

    solution = None
    for turn in range(CYCLES):
        solution = cycle(0, right_side, solution)
    return solution
```

```python
import jax
import jax.numpy as jnp
from jax import lax
from jax.experimental import pallas as pl
from jax.experimental.pallas import tpu as pltpu
from jax.sharding import PartitionSpec as P

CYCLES = 2
OMEGA = 0.7
F32 = jnp.float32
BF16 = jnp.bfloat16
MESH = pl.DeviceIdType.MESH

SIZE = ((16, 8, 128), (8, 4, 64), (4, 2, 32))
PLANES = (24, 16, 12)
LANES = (256, 128, 128)
REACH = (1, 1, 2)
ROWS = 16
HALO = 4
AXES = ("gx", "gy", "gz")
COUNT = {"gx": 4, "gy": 16, "gz": 8}

EXCHANGES = [(0, 3), (1, 2), (2, 2)]
for turn in range(CYCLES):
    EXCHANGES += [(1, 1), (2, 1), (2, 1), (1, 1)]
    if turn + 1 < CYCLES:
        EXCHANGES += [(0, 1)]


def exchange_scratch(level, fields):
    nx = SIZE[level][0]
    planes = PLANES[level]
    reach = REACH[level]
    copies = 4 + 2 * reach
    return [
        pltpu.VMEM((fields, nx, 8, 128), F32),
        pltpu.VMEM((2, fields, HALO, 8, 128), F32),
        pltpu.VMEM((fields, planes, 8, 128), F32),
        pltpu.VMEM((2 * reach, fields, planes, 8, 128), F32),
        pltpu.VMEM((2, fields, ROWS, 128), F32),
        pltpu.VMEM((2, fields, ROWS, 128), F32),
        pltpu.SemaphoreType.DMA((copies,)),
        pltpu.SemaphoreType.DMA((copies,)),
    ]


def coarse_scratch():
    return [
        pltpu.VMEM((16, 1, 128), F32),
        pltpu.VMEM((16, 1, 128), F32),
        pltpu.VMEM((1, 128), F32),
        pltpu.VMEM((4, 1, 128), F32),
        pltpu.VMEM((1, 128), F32),
        pltpu.VMEM((8, 1, 128), F32),
        pltpu.VMEM((16, 128), F32),
        pltpu.VMEM((16, 16, 128), F32),
        pltpu.SemaphoreType.DMA((41,)),
        pltpu.SemaphoreType.DMA((41,)),
    ]


PER_EXCHANGE = 8
PER_COARSE = 10


def peer(axis, step):
    return lax.rem(lax.axis_index(axis) + (step + COUNT[axis]), COUNT[axis])


def send(src, dst, send_sem, recv_sem, axis, step):
    copy = pltpu.make_async_remote_copy(
        src_ref=src,
        dst_ref=dst,
        send_sem=send_sem,
        recv_sem=recv_sem,
        device_id={axis: peer(axis, step)},
        device_id_type=MESH,
    )
    copy.start()
    return copy


def iota(shape, dim):
    return lax.broadcasted_iota(jnp.int32, shape, dim)


def turn_by(value, shift, axis):
    size = value.shape[axis]
    shift = shift % size
    if shift == 0:
        return value
    return pltpu.roll(value, shift, axis)


def exchange(jobs):
    copies = []
    for level, bufs, fields in jobs:
        own, from_x, _, _, _, _, ss, rs = bufs
        nx = SIZE[level][0]
        for i, value in enumerate(fields):
            own[i] = value
        copies.append(send(own.at[:, 0:HALO], from_x.at[0], ss.at[0], rs.at[0], "gx", -1))
        copies.append(send(own.at[:, nx - HALO : nx], from_x.at[1], ss.at[1], rs.at[1], "gx", 1))
    for copy in copies:
        copy.wait()
    copies = []
    for level, bufs, fields in jobs:
        own, from_x, slab, from_y, _, _, ss, rs = bufs
        nx = SIZE[level][0]
        for i in range(len(fields)):
            slab[i, 0:nx] = own[i]
            slab[i, nx : nx + HALO] = from_x[0, i]
            slab[i, nx + HALO : nx + 2 * HALO] = from_x[1, i]
        for step in range(1, REACH[level] + 1):
            for side, way in ((0, -1), (1, 1)):
                at = 2 * (step - 1) + side
                copies.append(send(slab, from_y.at[at], ss.at[2 + at], rs.at[2 + at], "gy", way * step))
    for copy in copies:
        copy.wait()
    copies = []
    columns = []
    for level, bufs, fields in jobs:
        _, _, slab, from_y, edges, from_z, ss, rs = bufs
        planes = PLANES[level]
        nz = SIZE[level][2]
        row = iota((planes, 8, 128), 1)
        lane = iota((ROWS, 128), 1)
        mine = []
        for i in range(len(fields)):
            value = slab[i]
            if level == 0:
                first = value
                second = jnp.where(row < 4, from_y[0, i], from_y[1, i])
            elif level == 1:
                first = jnp.where(row < 4, value, turn_by(from_y[0, i], 4, 1))
                second = turn_by(from_y[1, i], 4, 1)
            else:
                far = jnp.where(row < 4, turn_by(from_y[0, i], 2, 1), turn_by(from_y[2, i], 4, 1))
                first = jnp.where(row < 2, value, far)
                second = jnp.where(row < 6, turn_by(from_y[3, i], 4, 1), turn_by(from_y[1, i], 6, 1))
            column = jnp.concatenate([first, second], axis=1)
            mine.append(column)
            low = jnp.zeros((ROWS, 128), F32)
            high = jnp.zeros((ROWS, 128), F32)
            for p in range(planes):
                here = (lane >= 4 * p) & (lane < 4 * p + 4)
                low = jnp.where(here, turn_by(column[p], 4 * p, 1), low)
                high = jnp.where(here, turn_by(column[p], 4 * p - (nz - 4), 1), high)
            edges[0, i] = low
            edges[1, i] = high
        columns.append(mine)
        at = 2 + 2 * REACH[level]
        copies.append(send(edges.at[0], from_z.at[0], ss.at[at], rs.at[at], "gz", -1))
        copies.append(send(edges.at[1], from_z.at[1], ss.at[at + 1], rs.at[at + 1], "gz", 1))
    for copy in copies:
        copy.wait()
    rings = []
    for (level, bufs, fields), mine in zip(jobs, columns):
        from_z = bufs[5]
        planes = PLANES[level]
        nz = SIZE[level][2]
        lane = iota((ROWS, 128), 1)
        out = []
        for i in range(len(fields)):
            right = from_z[0, i]
            left = from_z[1, i]
            made = []
            for p in range(planes):
                after = turn_by(right, nz - 4 * p, 1)
                before = turn_by(left, 124 - 4 * p, 1)
                if level == 0:
                    side = jnp.where(lane < 64, after, before)
                    made.append(jnp.concatenate([mine[i][p], side], axis=1))
                else:
                    side = jnp.where(lane < 100, after, before)
                    made.append(jnp.where(lane < nz, mine[i][p], side))
            out.append(jnp.stack(made, axis=0))
        rings.append(out)
    return rings


def ring_offset(index, own, length):
    return jnp.where(index < own + HALO, index, index - length)


def inside(level):
    shape = (PLANES[level], ROWS, LANES[level])
    result = None
    for dim, axis in enumerate(AXES):
        own = SIZE[level][dim]
        off = ring_offset(iota(shape, dim), own, shape[dim])
        place = off + lax.axis_index(axis) * own
        good = (place >= 0) & (place < COUNT[axis] * own) & (off >= -HALO)
        result = good if result is None else result & good
    return result


def smooth_sum(value):
    total = 2.0 * value
    total = total + jnp.concatenate([value[1:], value[:1]], axis=0)
    total = total + jnp.concatenate([value[-1:], value[:-1]], axis=0)
    total = 2.0 * total + turn_by(total, 1, 1) + turn_by(total, -1, 1)
    total = 2.0 * total + turn_by(total, 1, 2) + turn_by(total, -1, 2)
    return 0.25 * total - 2.0 * value


def parts(value):
    high = value.astype(BF16)
    rest = value - high.astype(F32)
    mid = rest.astype(BF16)
    low = (rest - mid.astype(F32)).astype(BF16)
    return high, mid, low


def times_right(value, chosen):
    return sum(jnp.dot(piece, chosen, preferred_element_type=F32) for piece in parts(value))


def times_left(chosen, value):
    return sum(jnp.dot(chosen, piece, preferred_element_type=F32) for piece in parts(value))


def as_chosen(condition):
    return jnp.where(condition, 1.0, 0.0).astype(BF16)


def pool_matrices(level):
    nx, ny, nz = SIZE[level]
    shape = (nx * 4, nx * 8)
    i, j = iota(shape, 0), iota(shape, 1)
    x_match = (i >> 3) == (j >> 4)
    y_match = (i & 7) == ((j & 7) >> 1)
    rows = as_chosen(x_match & y_match & ((j & 7) < ny))
    i, j = iota((128, 128), 0), iota((128, 128), 1)
    lanes = as_chosen(((i >> 1) == j) & (i < nz))
    return rows, lanes


def pool(value, matrices):
    planes = value.shape[0]
    flat = value.reshape(planes * 8, 128)
    small = times_left(matrices[0], times_right(flat, matrices[1]))
    return small.reshape(planes // 2, 8, 128)


def coarse_index(index, level, dim, length, coarse_length):
    off = ring_offset(index, SIZE[level][dim], length) >> 1
    return jnp.where(off < 0, off + coarse_length, off)


def spread_matrices(level):
    shape = (PLANES[level] * ROWS, PLANES[level + 1] * ROWS)
    i, j = iota(shape, 0), iota(shape, 1)
    x_match = coarse_index(i >> 4, level, 0, PLANES[level], PLANES[level + 1]) == (j >> 4)
    y_match = coarse_index(i & 15, level, 1, ROWS, ROWS) == (j & 15)
    rows = as_chosen(x_match & y_match)
    shape = (128, LANES[level])
    i, j = iota(shape, 0), iota(shape, 1)
    lanes = as_chosen(coarse_index(j, level, 2, LANES[level], 128) == i)
    return rows, lanes


def spread(value, matrices, level):
    flat = value.reshape(PLANES[level + 1] * ROWS, 128)
    wide = times_left(matrices[0], times_right(flat, matrices[1]))
    return wide.reshape(PLANES[level], ROWS, LANES[level])


def kernel(f_ref, k_ref, m_ref, agg_ref, inverse_ref, out_ref, *scratch):
    n_ex = len(EXCHANGES) * PER_EXCHANGE
    ex_bufs = [scratch[PER_EXCHANGE * e : PER_EXCHANGE * (e + 1)] for e in range(len(EXCHANGES))]
    co_bufs = [scratch[n_ex + PER_COARSE * c : n_ex + PER_COARSE * (c + 1)] for c in range(CYCLES)]
    keep = scratch[n_ex + PER_COARSE * CYCLES :]
    coef = keep[0:15]
    onehot_lo, onehot_hi, state0, state1 = keep[15:19]
    source = keep[19:22]

    barrier = pltpu.get_barrier_semaphore()
    for axis in AXES:
        for step in range(1, COUNT[axis]):
            pl.semaphore_signal(barrier, inc=1, device_id={axis: peer(axis, step)}, device_id_type=MESH)
    pl.semaphore_wait(barrier, sum(COUNT[axis] - 1 for axis in AXES))

    pools = [pool_matrices(0), pool_matrices(1)]
    ks, ms = [k_ref[...]], [m_ref[...]]
    for level in range(2):
        ks.append(pool(ks[level], pools[level]) * 0.125)
        ms.append(pool(ms[level], pools[level]))
    used = iter(ex_bufs)
    rings = exchange(
        [
            (0, next(used), [ks[0], ms[0], f_ref[...]]),
            (1, next(used), [ks[1], ms[1]]),
            (2, next(used), [ks[2], ms[2]]),
        ]
    )
    for level in range(3):
        kp_ref, sk_ref, d_ref, g_ref, in_ref = coef[5 * level : 5 * level + 5]
        ok = inside(level)
        kp = jnp.where(ok, rings[level][0], 1.0)
        scaled = 2.0**level * kp
        diagonal = scaled * smooth_sum(kp) + rings[level][1]
        kp_ref[...] = kp
        sk_ref[...] = scaled
        d_ref[...] = diagonal
        g_ref[...] = jnp.where(ok, OMEGA / diagonal, 0.0)
        in_ref[...] = jnp.where(ok, 1.0, 0.0)
    source[0][...] = rings[0][2]

    lanes_of = iota((128, 128), 0)
    highs = iota((16, 128), 0)
    for i in range(8):
        row = agg_ref[i : i + 1, :]
        onehot_lo[:, 128 * i : 128 * i + 128] = as_chosen(((row & 127) == lanes_of) & (row >= 0))
        onehot_hi[:, 128 * i : 128 * i + 128] = jnp.where((row >> 7) == highs, 1.0, 0.0)

    def residual(level, value):
        kp_ref, sk_ref, d_ref, _, _ = coef[5 * level : 5 * level + 5]
        around = smooth_sum(kp_ref[...] * value)
        return source[level][...] - d_ref[...] * value + sk_ref[...] * around

    def sweep(level, value):
        return value + coef[5 * level + 3][...] * residual(level, value)

    def start(level):
        return coef[5 * level + 3][...] * source[level][...]

    def swap(level, block):
        return exchange([(level, next(used), [block])])[0][0]

    def aggregate_fix(rest, bufs):
        mine, from_gy, at_gy, from_gx, at_gx, from_gz, partial, pieces, ss, rs = bufs
        rows = [rest[i // 2, i % 2 : i % 2 + 1, :] for i in range(8)]
        left = jnp.concatenate([onehot_hi[:, 128 * i : 128 * i + 128] * rows[i] for i in range(8)], axis=1)
        sums = sum(
            lax.dot_general(piece, onehot_lo[...], (((1,), (1,)), ((), ())), preferred_element_type=F32)
            for piece in parts(left)
        )
        for j in range(16):
            mine[j] = sums[j : j + 1, :]
        copies = []
        for step in range(1, 16):
            copies.append(send(mine.at[peer("gy", step)], from_gy.at[step], ss.at[step], rs.at[step], "gy", step))
        for copy in copies:
            copy.wait()
        total = mine[lax.axis_index("gy")]
        for step in range(1, 16):
            total = total + from_gy[step]
        at_gy[...] = total
        copies = []
        for step in range(1, 4):
            copies.append(send(at_gy, from_gx.at[step], ss.at[15 + step], rs.at[15 + step], "gx", step))
        for copy in copies:
            copy.wait()
        for step in range(1, 4):
            total = total + from_gx[step]
        at_gx[...] = total
        copies = []
        for step in range(1, 8):
            copies.append(send(at_gx, from_gz.at[step], ss.at[18 + step], rs.at[18 + step], "gz", step))
        for copy in copies:
            copy.wait()
        for step in range(1, 8):
            total = total + from_gz[step]
        down = jnp.broadcast_to(total, (128, 128)).T
        for j in range(16):
            product = down * inverse_ref[:, 128 * j : 128 * j + 128]
            partial[j : j + 1, :] = jnp.sum(product, axis=0, keepdims=True)
        copies = []
        for step in range(1, 16):
            at = 25 + step
            copies.append(send(partial, pieces.at[step], ss.at[at], rs.at[at], "gy", step))
        for copy in copies:
            copy.wait()
        fixes = partial[...]
        for step in range(1, 16):
            fixes = fixes + pieces[step]
        wide = times_right(fixes, onehot_lo[...])
        cells = jnp.sum(wide * onehot_hi[...], axis=0, keepdims=True)
        row = iota((8, 128), 0)
        planes = []
        for x in range(4):
            even = cells[:, 256 * x : 256 * x + 128]
            odd = cells[:, 256 * x + 128 : 256 * x + 256]
            planes.append(jnp.where(row == 0, even, jnp.where(row == 1, odd, 0.0)))
        return jnp.stack(planes, axis=0)

    value = start(0)
    for turn in range(CYCLES):
        if turn > 0:
            value = sweep(0, value)
        value = sweep(0, value)
        rest = residual(0, value)[0:16, 0:8, 0:128]
        state0[...] = value
        source[1][...] = swap(1, pool(rest, pools[0]))
        value = sweep(1, start(1))
        rest = residual(1, value)[0:8, 0:8, :]
        state1[...] = value
        source[2][...] = swap(2, pool(rest, pools[1]))
        value = sweep(2, start(2))
        rest = residual(2, value)[0:4, 0:8, :]
        fixed = value[0:4, 0:8, :] + aggregate_fix(rest, co_bufs[turn])
        value = swap(2, fixed) * coef[14][...]
        value = sweep(2, sweep(2, value))
        value = state1[...] + spread(value, spread_matrices(1), 1)
        value = sweep(1, sweep(1, value))
        value = swap(1, value[0:8, 0:8, :]) * coef[9][...]
        value = state0[...] + spread(value, spread_matrices(0), 0)
        value = sweep(0, sweep(0, value))
        if turn + 1 < CYCLES:
            value = swap(0, value[0:16, 0:8, 0:128]) * coef[4][...]
    out_ref[...] = value[0:16, 0:8, 0:128]


def local(right_side, conduct, mass, aggregate_of, coarse_inverse):
    agg = jnp.pad(aggregate_of.reshape(8, 32), ((0, 0), (0, 96)), constant_values=-1)
    scratch = []
    for level, fields in EXCHANGES:
        scratch += exchange_scratch(level, fields)
    for _ in range(CYCLES):
        scratch += coarse_scratch()
    rings = [pltpu.VMEM((PLANES[level], ROWS, LANES[level]), F32) for level in range(3)]
    for ring in rings:
        scratch += [ring] * 5
    scratch += [pltpu.VMEM((128, 1024), BF16), pltpu.VMEM((16, 1024), F32), rings[0], rings[1]]
    scratch += rings
    return pl.pallas_call(
        kernel,
        out_shape=jax.ShapeDtypeStruct(right_side.shape, F32),
        in_specs=[pl.BlockSpec(memory_space=pltpu.VMEM)] * 5,
        out_specs=pl.BlockSpec(memory_space=pltpu.VMEM),
        scratch_shapes=scratch,
        compiler_params=pltpu.CompilerParams(collective_id=0, has_side_effects=True),
    )(right_side, conduct, mass, agg, coarse_inverse)


def solution(mesh):
    return jax.shard_map(
        local,
        mesh=mesh,
        in_specs=(
            P("gx", "gy", "gz"),
            P("gx", "gy", "gz"),
            P("gx", "gy", "gz"),
            P("gx", "gy", "gz"),
            P("gy", None),
        ),
        out_specs=P("gx", "gy", "gz"),
        check_vma=False,
    )
```

```python
import jax
import jax.numpy as jnp
from jax import lax
from jax.experimental import pallas as pl
from jax.experimental.pallas import tpu as pltpu
from jax.sharding import PartitionSpec as P

CYCLES = 2
OMEGA = 0.7
F32 = jnp.float32
BF16 = jnp.bfloat16
MESH = pl.DeviceIdType.MESH

SIZE = ((16, 8, 128), (8, 4, 64), (4, 2, 32))
PLANES = (24, 16, 12)
LANES = (256, 128, 128)
REACH = (1, 1, 2)
ROWS = 16
HALO = 4
AXES = ("gx", "gy", "gz")
COUNT = {"gx": 4, "gy": 16, "gz": 8}

EXCHANGES = [(0, 3), (1, 2), (2, 2)]
for turn in range(CYCLES):
    EXCHANGES += [(1, 1), (2, 1), (2, 1), (1, 1)]
    if turn + 1 < CYCLES:
        EXCHANGES += [(0, 1)]


def neighbours(level):
    reach = REACH[level]
    steps = [(x, y, z) for x in (-1, 0, 1) for y in range(-reach, reach + 1) for z in (-1, 0, 1)]
    return [step for step in steps if step != (0, 0, 0)]


def exchange_scratch(level, fields):
    nx = SIZE[level][0]
    planes = PLANES[level]
    reach = REACH[level]
    copies = len(neighbours(level))
    return [
        pltpu.VMEM((fields, nx, 8, 128), F32),
        pltpu.VMEM((2, fields, HALO, 8, 128), F32),
        pltpu.VMEM((2 * reach, fields, planes, 8, 128), F32),
        pltpu.VMEM((2, fields, 8, 128), F32),
        pltpu.VMEM((2, 3, 2 * reach + 1, fields, 8, 128), F32),
        pltpu.SemaphoreType.DMA((copies,)),
        pltpu.SemaphoreType.DMA((copies,)),
    ]


def coarse_scratch():
    return [
        pltpu.VMEM((16, 1, 128), F32),
        pltpu.VMEM((16, 1, 128), F32),
        pltpu.VMEM((1, 128), F32),
        pltpu.VMEM((4, 1, 128), F32),
        pltpu.VMEM((1, 128), F32),
        pltpu.VMEM((8, 1, 128), F32),
        pltpu.VMEM((16, 128), F32),
        pltpu.VMEM((16, 16, 128), F32),
        pltpu.SemaphoreType.DMA((41,)),
        pltpu.SemaphoreType.DMA((41,)),
    ]


PER_EXCHANGE = 7
PER_COARSE = 10


def peer(axis, step):
    return lax.rem(lax.axis_index(axis) + (step + COUNT[axis]), COUNT[axis])


def send_to(src, dst, send_sem, recv_sem, steps):
    copy = pltpu.make_async_remote_copy(
        src_ref=src,
        dst_ref=dst,
        send_sem=send_sem,
        recv_sem=recv_sem,
        device_id={axis: peer(axis, step) for axis, step in zip(AXES, steps) if step != 0},
        device_id_type=MESH,
    )
    copy.start()
    return copy


def send(src, dst, send_sem, recv_sem, axis, step):
    return send_to(src, dst, send_sem, recv_sem, [step if axis == name else 0 for name in AXES])


def iota(shape, dim):
    return lax.broadcasted_iota(jnp.int32, shape, dim)


def turn_by(value, shift, axis):
    size = value.shape[axis]
    shift = shift % size
    if shift == 0:
        return value
    return pltpu.roll(value, shift, axis)


def slab_of(step):
    return 2 * (abs(step) - 1) + (0 if step > 0 else 1)


def join_rows(level, value, near):
    row = iota(value.shape, 1)
    if level == 0:
        first = value
        second = jnp.where(row < 4, near(1), near(-1))
    elif level == 1:
        first = jnp.where(row < 4, value, turn_by(near(1), 4, 1))
        second = turn_by(near(-1), 4, 1)
    else:
        far = jnp.where(row < 4, turn_by(near(1), 2, 1), turn_by(near(2), 4, 1))
        first = jnp.where(row < 2, value, far)
        second = jnp.where(row < 6, turn_by(near(-2), 4, 1), turn_by(near(-1), 6, 1))
    return jnp.concatenate([first, second], axis=1)


def exchange(jobs):
    copies = []
    for level, bufs, fields in jobs:
        own, from_x, from_y, edges, from_z, ss, rs = bufs
        nx, _, nz = SIZE[level]
        reach = REACH[level]
        lane = iota((8, 128), 1)
        for i, value in enumerate(fields):
            own[i] = value
            low = jnp.zeros((8, 128), F32)
            high = jnp.zeros((8, 128), F32)
            for p in range(nx):
                here = (lane >= 4 * p) & (lane < 4 * p + 4)
                low = jnp.where(here, turn_by(value[p], 4 * p, 1), low)
                high = jnp.where(here, turn_by(value[p], 4 * p - (nz - 4), 1), high)
            edges[0, i] = low
            edges[1, i] = high
        order = sorted(enumerate(neighbours(level)), key=lambda item: -sum(abs(step) for step in item[1]))
        for at, (dx, dy, dz) in order:
            part = pl.ds(0, nx) if dx == 0 else pl.ds(0, HALO) if dx < 0 else pl.ds(nx - HALO, HALO)
            there = pl.ds(0, nx) if dx == 0 else pl.ds(nx, HALO) if dx < 0 else pl.ds(nx + HALO, HALO)
            if dz != 0:
                side = 0 if dz < 0 else 1
                src, dst = edges.at[side], from_z.at[side, 1 - dx, reach - dy]
            elif dy != 0:
                src, dst = own.at[:, part], from_y.at[slab_of(-dy), :, there]
            else:
                src, dst = own.at[:, part], from_x.at[0 if dx < 0 else 1]
            copies.append(send_to(src, dst, ss.at[at], rs.at[at], (dx, dy, dz)))
    for copy in copies:
        copy.wait()
    rings = []
    for level, bufs, fields in jobs:
        own, from_x, from_y, edges, from_z, ss, rs = bufs
        nx, _, nz = SIZE[level]
        reach = REACH[level]
        planes = PLANES[level]
        lane = iota((ROWS, 128), 1)
        out = []
        for i in range(len(fields)):
            block = jnp.concatenate([own[i], from_x[0, i], from_x[1, i]], axis=0)
            column = join_rows(level, block, lambda step: from_y[slab_of(step), i])
            packed = [
                [
                    join_rows(
                        level,
                        from_z[side, x, reach, i][None],
                        lambda step: from_z[side, x, reach + step, i][None],
                    )[0]
                    for x in range(3)
                ]
                for side in range(2)
            ]
            made = []
            for p in range(planes):
                x, base = (1, p) if p < nx else (2, p - nx) if p < nx + HALO else (0, p - 2 * HALO)
                after = turn_by(packed[0][x], nz - 4 * base, 1)
                before = turn_by(packed[1][x], 124 - 4 * base, 1)
                if level == 0:
                    made.append(jnp.concatenate([column[p], jnp.where(lane < 64, after, before)], axis=1))
                else:
                    made.append(jnp.where(lane < nz, column[p], jnp.where(lane < 100, after, before)))
            out.append(jnp.stack(made, axis=0))
        rings.append(out)
    return rings


def ring_offset(index, own, length):
    return jnp.where(index < own + HALO, index, index - length)


def inside(level):
    shape = (PLANES[level], ROWS, LANES[level])
    result = None
    for dim, axis in enumerate(AXES):
        own = SIZE[level][dim]
        off = ring_offset(iota(shape, dim), own, shape[dim])
        place = off + lax.axis_index(axis) * own
        good = (place >= 0) & (place < COUNT[axis] * own) & (off >= -HALO)
        result = good if result is None else result & good
    return result


def smooth_sum(value):
    total = 2.0 * value
    total = total + jnp.concatenate([value[1:], value[:1]], axis=0)
    total = total + jnp.concatenate([value[-1:], value[:-1]], axis=0)
    total = 2.0 * total + turn_by(total, 1, 1) + turn_by(total, -1, 1)
    total = 2.0 * total + turn_by(total, 1, 2) + turn_by(total, -1, 2)
    return 0.25 * total - 2.0 * value


def parts(value):
    high = value.astype(BF16)
    rest = value - high.astype(F32)
    mid = rest.astype(BF16)
    low = (rest - mid.astype(F32)).astype(BF16)
    return high, mid, low


def times_right(value, chosen):
    return sum(jnp.dot(piece, chosen, preferred_element_type=F32) for piece in parts(value))


def times_left(chosen, value):
    return sum(jnp.dot(chosen, piece, preferred_element_type=F32) for piece in parts(value))


def as_chosen(condition):
    return jnp.where(condition, 1.0, 0.0).astype(BF16)


def pool_matrices(level):
    nx, ny, nz = SIZE[level]
    shape = (nx * 4, nx * 8)
    i, j = iota(shape, 0), iota(shape, 1)
    x_match = (i >> 3) == (j >> 4)
    y_match = (i & 7) == ((j & 7) >> 1)
    rows = as_chosen(x_match & y_match & ((j & 7) < ny))
    i, j = iota((128, 128), 0), iota((128, 128), 1)
    lanes = as_chosen(((i >> 1) == j) & (i < nz))
    return rows, lanes


def pool(value, matrices):
    planes = value.shape[0]
    flat = value.reshape(planes * 8, 128)
    small = times_left(matrices[0], times_right(flat, matrices[1]))
    return small.reshape(planes // 2, 8, 128)


def coarse_index(index, level, dim, length, coarse_length):
    off = ring_offset(index, SIZE[level][dim], length) >> 1
    return jnp.where(off < 0, off + coarse_length, off)


def spread_matrices(level):
    shape = (PLANES[level] * ROWS, PLANES[level + 1] * ROWS)
    i, j = iota(shape, 0), iota(shape, 1)
    x_match = coarse_index(i >> 4, level, 0, PLANES[level], PLANES[level + 1]) == (j >> 4)
    y_match = coarse_index(i & 15, level, 1, ROWS, ROWS) == (j & 15)
    rows = as_chosen(x_match & y_match)
    shape = (128, LANES[level])
    i, j = iota(shape, 0), iota(shape, 1)
    lanes = as_chosen(coarse_index(j, level, 2, LANES[level], 128) == i)
    return rows, lanes


def spread(value, matrices, level):
    flat = value.reshape(PLANES[level + 1] * ROWS, 128)
    wide = times_left(matrices[0], times_right(flat, matrices[1]))
    return wide.reshape(PLANES[level], ROWS, LANES[level])


def all_peers():
    steps = neighbours(2)
    steps += [(0, step, 0) for step in range(1, 16)]
    steps += [(step, 0, 0) for step in range(1, 4)]
    steps += [(0, 0, step) for step in range(1, 8)]
    return {tuple(step % COUNT[axis] for axis, step in zip(AXES, triple)) for triple in steps}


def kernel(f_ref, k_ref, m_ref, agg_ref, inverse_ref, out_ref, *scratch):
    n_ex = len(EXCHANGES) * PER_EXCHANGE
    ex_bufs = [scratch[PER_EXCHANGE * e : PER_EXCHANGE * (e + 1)] for e in range(len(EXCHANGES))]
    co_bufs = [scratch[n_ex + PER_COARSE * c : n_ex + PER_COARSE * (c + 1)] for c in range(CYCLES)]
    keep = scratch[n_ex + PER_COARSE * CYCLES :]
    coef = keep[0:15]
    onehot_lo, onehot_hi, state0, state1 = keep[15:19]
    source = keep[19:22]

    barrier = pltpu.get_barrier_semaphore()
    greeted = sorted(all_peers())
    for steps in greeted:
        target = {axis: peer(axis, step) for axis, step in zip(AXES, steps) if step != 0}
        pl.semaphore_signal(barrier, inc=1, device_id=target, device_id_type=MESH)
    pl.semaphore_wait(barrier, len(greeted))

    pools = [pool_matrices(0), pool_matrices(1)]
    ks, ms = [k_ref[...]], [m_ref[...]]
    for level in range(2):
        ks.append(pool(ks[level], pools[level]) * 0.125)
        ms.append(pool(ms[level], pools[level]))
    used = iter(ex_bufs)
    rings = exchange(
        [
            (0, next(used), [ks[0], ms[0], f_ref[...]]),
            (1, next(used), [ks[1], ms[1]]),
            (2, next(used), [ks[2], ms[2]]),
        ]
    )
    for level in range(3):
        kp_ref, sk_ref, d_ref, g_ref, in_ref = coef[5 * level : 5 * level + 5]
        ok = inside(level)
        kp = jnp.where(ok, rings[level][0], 1.0)
        scaled = 2.0**level * kp
        diagonal = scaled * smooth_sum(kp) + rings[level][1]
        kp_ref[...] = kp
        sk_ref[...] = scaled
        d_ref[...] = diagonal
        g_ref[...] = jnp.where(ok, OMEGA / diagonal, 0.0)
        in_ref[...] = jnp.where(ok, 1.0, 0.0)
    source[0][...] = rings[0][2]

    lanes_of = iota((128, 128), 0)
    highs = iota((16, 128), 0)
    for i in range(8):
        row = agg_ref[i : i + 1, :]
        onehot_lo[:, 128 * i : 128 * i + 128] = as_chosen(((row & 127) == lanes_of) & (row >= 0))
        onehot_hi[:, 128 * i : 128 * i + 128] = jnp.where((row >> 7) == highs, 1.0, 0.0)

    def residual(level, value):
        kp_ref, sk_ref, d_ref, _, _ = coef[5 * level : 5 * level + 5]
        around = smooth_sum(kp_ref[...] * value)
        return source[level][...] - d_ref[...] * value + sk_ref[...] * around

    def sweep(level, value):
        return value + coef[5 * level + 3][...] * residual(level, value)

    def start(level):
        return coef[5 * level + 3][...] * source[level][...]

    def swap(level, block):
        return exchange([(level, next(used), [block])])[0][0]

    def aggregate_fix(rest, bufs):
        mine, from_gy, at_gy, from_gx, at_gx, from_gz, partial, pieces, ss, rs = bufs
        rows = [rest[i // 2, i % 2 : i % 2 + 1, :] for i in range(8)]
        left = jnp.concatenate([onehot_hi[:, 128 * i : 128 * i + 128] * rows[i] for i in range(8)], axis=1)
        sums = sum(
            lax.dot_general(piece, onehot_lo[...], (((1,), (1,)), ((), ())), preferred_element_type=F32)
            for piece in parts(left)
        )
        for j in range(16):
            mine[j] = sums[j : j + 1, :]
        copies = []
        for step in range(1, 16):
            copies.append(send(mine.at[peer("gy", step)], from_gy.at[step], ss.at[step], rs.at[step], "gy", step))
        for copy in copies:
            copy.wait()
        total = mine[lax.axis_index("gy")]
        for step in range(1, 16):
            total = total + from_gy[step]
        at_gy[...] = total
        copies = []
        for step in range(1, 4):
            copies.append(send(at_gy, from_gx.at[step], ss.at[15 + step], rs.at[15 + step], "gx", step))
        for copy in copies:
            copy.wait()
        for step in range(1, 4):
            total = total + from_gx[step]
        at_gx[...] = total
        copies = []
        for step in range(1, 8):
            copies.append(send(at_gx, from_gz.at[step], ss.at[18 + step], rs.at[18 + step], "gz", step))
        for copy in copies:
            copy.wait()
        for step in range(1, 8):
            total = total + from_gz[step]
        down = jnp.broadcast_to(total, (128, 128)).T
        for j in range(16):
            product = down * inverse_ref[:, 128 * j : 128 * j + 128]
            partial[j : j + 1, :] = jnp.sum(product, axis=0, keepdims=True)
        copies = []
        for step in range(1, 16):
            at = 25 + step
            copies.append(send(partial, pieces.at[step], ss.at[at], rs.at[at], "gy", step))
        for copy in copies:
            copy.wait()
        fixes = partial[...]
        for step in range(1, 16):
            fixes = fixes + pieces[step]
        wide = times_right(fixes, onehot_lo[...])
        cells = jnp.sum(wide * onehot_hi[...], axis=0, keepdims=True)
        row = iota((8, 128), 0)
        planes = []
        for x in range(4):
            even = cells[:, 256 * x : 256 * x + 128]
            odd = cells[:, 256 * x + 128 : 256 * x + 256]
            planes.append(jnp.where(row == 0, even, jnp.where(row == 1, odd, 0.0)))
        return jnp.stack(planes, axis=0)

    value = start(0)
    for turn in range(CYCLES):
        if turn > 0:
            value = sweep(0, value)
        value = sweep(0, value)
        rest = residual(0, value)[0:16, 0:8, 0:128]
        state0[...] = value
        source[1][...] = swap(1, pool(rest, pools[0]))
        value = sweep(1, start(1))
        rest = residual(1, value)[0:8, 0:8, :]
        state1[...] = value
        source[2][...] = swap(2, pool(rest, pools[1]))
        value = sweep(2, start(2))
        rest = residual(2, value)[0:4, 0:8, :]
        fixed = value[0:4, 0:8, :] + aggregate_fix(rest, co_bufs[turn])
        value = swap(2, fixed) * coef[14][...]
        value = sweep(2, sweep(2, value))
        value = state1[...] + spread(value, spread_matrices(1), 1)
        value = sweep(1, sweep(1, value))
        value = swap(1, value[0:8, 0:8, :]) * coef[9][...]
        value = state0[...] + spread(value, spread_matrices(0), 0)
        value = sweep(0, sweep(0, value))
        if turn + 1 < CYCLES:
            value = swap(0, value[0:16, 0:8, 0:128]) * coef[4][...]
    out_ref[...] = value[0:16, 0:8, 0:128]


def local(right_side, conduct, mass, aggregate_of, coarse_inverse):
    agg = jnp.pad(aggregate_of.reshape(8, 32), ((0, 0), (0, 96)), constant_values=-1)
    scratch = []
    for level, fields in EXCHANGES:
        scratch += exchange_scratch(level, fields)
    for _ in range(CYCLES):
        scratch += coarse_scratch()
    rings = [pltpu.VMEM((PLANES[level], ROWS, LANES[level]), F32) for level in range(3)]
    for ring in rings:
        scratch += [ring] * 5
    scratch += [pltpu.VMEM((128, 1024), BF16), pltpu.VMEM((16, 1024), F32), rings[0], rings[1]]
    scratch += rings
    return pl.pallas_call(
        kernel,
        out_shape=jax.ShapeDtypeStruct(right_side.shape, F32),
        in_specs=[pl.BlockSpec(memory_space=pltpu.VMEM)] * 5,
        out_specs=pl.BlockSpec(memory_space=pltpu.VMEM),
        scratch_shapes=scratch,
        compiler_params=pltpu.CompilerParams(collective_id=0, has_side_effects=True),
    )(right_side, conduct, mass, agg, coarse_inverse)


def solution(mesh):
    return jax.shard_map(
        local,
        mesh=mesh,
        in_specs=(
            P("gx", "gy", "gz"),
            P("gx", "gy", "gz"),
            P("gx", "gy", "gz"),
            P("gx", "gy", "gz"),
            P("gy", None),
        ),
        out_specs=P("gx", "gy", "gz"),
        check_vma=False,
    )
```

```python
import jax
import jax.numpy as jnp
from jax import lax
from jax.experimental import pallas as pl
from jax.experimental.pallas import tpu as pltpu
from jax.sharding import PartitionSpec as P

CYCLES = 2
OMEGA = 0.7
F32 = jnp.float32
BF16 = jnp.bfloat16
MESH = pl.DeviceIdType.MESH

SIZE = ((16, 8, 128), (8, 4, 64), (4, 2, 32))
PLANES = (24, 16, 12)
LANES = (256, 128, 128)
REACH = (1, 1, 2)
ROWS = 16
HALO = 4
AXES = ("gx", "gy", "gz")
COUNT = {"gx": 4, "gy": 16, "gz": 8}

EXCHANGES = [(0, 3), (1, 2), (2, 2)]
for turn in range(CYCLES):
    EXCHANGES += [(1, 1), (2, 1), (2, 1), (1, 1)]
    if turn + 1 < CYCLES:
        EXCHANGES += [(0, 1)]


def neighbours(level):
    reach = REACH[level]
    steps = [(x, y, z) for x in (-1, 0, 1) for y in range(-reach, reach + 1) for z in (-1, 0, 1)]
    return [step for step in steps if step != (0, 0, 0)]


def exchange_scratch(level, fields):
    nx = SIZE[level][0]
    planes = PLANES[level]
    copies = len(neighbours(level))
    sems = [pltpu.SemaphoreType.DMA((copies,)), pltpu.SemaphoreType.DMA((copies,))]
    edges = [pltpu.VMEM((2, fields, 8, 128), F32), pltpu.VMEM((2, 3, 3, fields, 8, 128), F32)]
    if level == 2:
        nothing = pltpu.VMEM((8, 128), F32)
        return [
            pltpu.VMEM((fields, 8, 128), F32),
            pltpu.VMEM((3, 5, 3, fields, 8, 128), F32),
            nothing,
            nothing,
            nothing,
        ] + sems
    if level == 1:
        return [
            pltpu.VMEM((2, fields, 8, 128), F32),
            pltpu.VMEM((3, 3, 2, fields, 8, 128), F32),
            pltpu.VMEM((8, 128), F32),
        ] + edges + sems
    return [
        pltpu.VMEM((fields, nx, 8, 128), F32),
        pltpu.VMEM((2, fields, HALO, 8, 128), F32),
        pltpu.VMEM((2, fields, planes, 8, 128), F32),
    ] + edges + sems


def coarse_scratch():
    return [
        pltpu.VMEM((16, 1, 128), F32),
        pltpu.VMEM((16, 1, 128), F32),
        pltpu.VMEM((1, 128), F32),
        pltpu.VMEM((32, 1, 128), F32),
        pltpu.VMEM((16, 128), F32),
        pltpu.VMEM((16, 16, 128), F32),
        pltpu.SemaphoreType.DMA((62,)),
        pltpu.SemaphoreType.DMA((62,)),
    ]


PER_EXCHANGE = 7
PER_COARSE = 8


def peer(axis, step):
    return lax.rem(lax.axis_index(axis) + (step + COUNT[axis]), COUNT[axis])


def send_to(src, dst, send_sem, recv_sem, steps):
    copy = pltpu.make_async_remote_copy(
        src_ref=src,
        dst_ref=dst,
        send_sem=send_sem,
        recv_sem=recv_sem,
        device_id={axis: peer(axis, step) for axis, step in zip(AXES, steps) if step != 0},
        device_id_type=MESH,
    )
    copy.start()
    return copy


def send(src, dst, send_sem, recv_sem, axis, step):
    return send_to(src, dst, send_sem, recv_sem, [step if axis == name else 0 for name in AXES])


def iota(shape, dim):
    return lax.broadcasted_iota(jnp.int32, shape, dim)


def turn_by(value, shift, axis):
    size = value.shape[axis]
    shift = shift % size
    if shift == 0:
        return value
    return pltpu.roll(value, shift, axis)


def slab_of(step):
    return 2 * (abs(step) - 1) + (0 if step > 0 else 1)


def join_rows(level, value, near):
    row = iota(value.shape, 1)
    if level == 0:
        first = value
        second = jnp.where(row < 4, near(1), near(-1))
    elif level == 1:
        first = jnp.where(row < 4, value, turn_by(near(1), 4, 1))
        second = turn_by(near(-1), 4, 1)
    else:
        far = jnp.where(row < 4, turn_by(near(1), 2, 1), turn_by(near(2), 4, 1))
        first = jnp.where(row < 2, value, far)
        second = jnp.where(row < 6, turn_by(near(-2), 4, 1), turn_by(near(-1), 6, 1))
    return jnp.concatenate([first, second], axis=1)


def pack_edges(value, edges, i, nx, nz):
    lane = iota((8, 128), 1)
    low = jnp.zeros((8, 128), F32)
    high = jnp.zeros((8, 128), F32)
    for p in range(nx):
        here = (lane >= 4 * p) & (lane < 4 * p + 4)
        low = jnp.where(here, turn_by(value[p], 4 * p, 1), low)
        high = jnp.where(here, turn_by(value[p], 4 * p - (nz - 4), 1), high)
    edges[0, i] = low
    edges[1, i] = high


def pack_block(level, value):
    lane = iota((8, 128), 1)
    row = iota((8, 128), 0)
    tiles = []
    for base in range(0, SIZE[level][0], 4):
        if level == 2:
            tile = value[base]
            for q in range(1, 4):
                tile = jnp.where(lane < 32 * q, tile, turn_by(value[base + q], 32 * q, 1))
        else:
            upper = jnp.where(lane < 64, value[base], turn_by(value[base + 1], 64, 1))
            lower = jnp.where(lane < 64, value[base + 2], turn_by(value[base + 3], 64, 1))
            tile = jnp.where(row < 4, upper, turn_by(lower, 4, 0))
        tiles.append(tile)
    return tiles


def unpack_tile(tile, q):
    return turn_by(turn_by(tile, -64 * (q % 2), 1), -4 * (q // 2), 0)


def exchange(jobs, meanwhile=None):
    copies = []
    for level, bufs, fields in jobs:
        own, near, from_y, edges, from_z, ss, rs = bufs
        nx, _, nz = SIZE[level]
        reach = REACH[level]
        for i, value in enumerate(fields):
            if level == 0:
                own[i] = value
            elif level == 1:
                for t, tile in enumerate(pack_block(1, value)):
                    own[t, i] = tile
            else:
                own[i] = pack_block(2, value)[0]
            if level < 2:
                pack_edges(value, edges, i, nx, nz)
        order = sorted(enumerate(neighbours(level)), key=lambda item: -sum(abs(step) for step in item[1]))
        for at, (dx, dy, dz) in order:
            part = pl.ds(0, nx) if dx == 0 else pl.ds(0, HALO) if dx < 0 else pl.ds(nx - HALO, HALO)
            there = pl.ds(0, nx) if dx == 0 else pl.ds(nx, HALO) if dx < 0 else pl.ds(nx + HALO, HALO)
            if level == 2:
                src, dst = own, near.at[1 - dx, reach - dy, 1 - dz]
            elif dz != 0:
                side = 0 if dz < 0 else 1
                src, dst = edges.at[side], from_z.at[side, 1 - dx, reach - dy]
            elif level == 1:
                if dx == 0:
                    src, dst = own, near.at[1, 1 - dy]
                else:
                    src, dst = own.at[0 if dx < 0 else 1], near.at[1 - dx, 1 - dy, 0]
            elif dy != 0:
                src, dst = own.at[:, part], from_y.at[slab_of(-dy), :, there]
            else:
                src, dst = own.at[:, part], near.at[0 if dx < 0 else 1]
            copies.append(send_to(src, dst, ss.at[at], rs.at[at], (dx, dy, dz)))
    if meanwhile is not None:
        meanwhile()
    for copy in copies:
        copy.wait()
    rings = []
    for level, bufs, fields in jobs:
        own, near, from_y, edges, from_z, ss, rs = bufs
        nx, _, nz = SIZE[level]
        planes = PLANES[level]
        lane = iota((ROWS, 128), 1)
        out = []
        for i, value in enumerate(fields):
            made = []
            places = [(1, p) if p < nx else (2, p - nx) if p < nx + HALO else (0, p - 2 * HALO) for p in range(planes)]
            if level == 2:

                def tile_of(x, step, z):
                    return (own[i] if (x, step, z) == (1, 0, 1) else near[x, 2 + step, z, i])[None]

                tiles = [
                    [join_rows(2, tile_of(x, 0, z), lambda step: tile_of(x, step, z))[0] for z in range(3)]
                    for x in range(3)
                ]
                for x, q in places:
                    middle = turn_by(tiles[x][1], -32 * q, 1)
                    after = turn_by(tiles[x][2], 32 - 32 * q, 1)
                    before = turn_by(tiles[x][0], 96 - 32 * q, 1)
                    made.append(jnp.where(lane < 32, middle, jnp.where(lane < 100, after, before)))
                out.append(jnp.stack(made, axis=0))
                continue
            if level == 1:

                def slab(step):
                    parts_of = [value[p] for p in range(nx)] if step == 0 else [
                        unpack_tile(near[1, 1 + step, p // 4, i], p % 4) for p in range(nx)
                    ]
                    for x in (2, 0):
                        parts_of += [unpack_tile(near[x, 1 + step, 0, i], q) for q in range(4)]
                    return jnp.stack(parts_of, axis=0)

                column = join_rows(1, slab(0), slab)
            else:
                block = jnp.concatenate([own[i], near[0, i], near[1, i]], axis=0)
                column = join_rows(0, block, lambda step: from_y[slab_of(step), i])
            packed = [
                [
                    join_rows(level, from_z[side, x, 1, i][None], lambda step: from_z[side, x, 1 + step, i][None])[0]
                    for x in range(3)
                ]
                for side in range(2)
            ]
            for p, (x, base) in enumerate(places):
                after = turn_by(packed[0][x], nz - 4 * base, 1)
                before = turn_by(packed[1][x], 124 - 4 * base, 1)
                if level == 0:
                    made.append(jnp.concatenate([column[p], jnp.where(lane < 64, after, before)], axis=1))
                else:
                    made.append(jnp.where(lane < nz, column[p], jnp.where(lane < 100, after, before)))
            out.append(jnp.stack(made, axis=0))
        rings.append(out)
    return rings


def ring_offset(index, own, length):
    return jnp.where(index < own + HALO, index, index - length)


def inside(level):
    shape = (PLANES[level], ROWS, LANES[level])
    result = None
    for dim, axis in enumerate(AXES):
        own = SIZE[level][dim]
        off = ring_offset(iota(shape, dim), own, shape[dim])
        place = off + lax.axis_index(axis) * own
        good = (place >= 0) & (place < COUNT[axis] * own) & (off >= -HALO)
        result = good if result is None else result & good
    return result


def smooth_sum(value):
    total = 2.0 * value
    total = total + jnp.concatenate([value[1:], value[:1]], axis=0)
    total = total + jnp.concatenate([value[-1:], value[:-1]], axis=0)
    total = 2.0 * total + turn_by(total, 1, 1) + turn_by(total, -1, 1)
    total = 2.0 * total + turn_by(total, 1, 2) + turn_by(total, -1, 2)
    return 0.25 * total - 2.0 * value


def parts(value):
    high = value.astype(BF16)
    rest = value - high.astype(F32)
    mid = rest.astype(BF16)
    low = (rest - mid.astype(F32)).astype(BF16)
    return high, mid, low


def times_right(value, chosen):
    return sum(jnp.dot(piece, chosen, preferred_element_type=F32) for piece in parts(value))


def times_left(chosen, value):
    return sum(jnp.dot(chosen, piece, preferred_element_type=F32) for piece in parts(value))


def as_chosen(condition):
    return jnp.where(condition, 1.0, 0.0).astype(BF16)


def pool_matrices(level):
    nx, ny, nz = SIZE[level]
    shape = (nx * 4, nx * 8)
    i, j = iota(shape, 0), iota(shape, 1)
    x_match = (i >> 3) == (j >> 4)
    y_match = (i & 7) == ((j & 7) >> 1)
    rows = as_chosen(x_match & y_match & ((j & 7) < ny))
    i, j = iota((128, 128), 0), iota((128, 128), 1)
    lanes = as_chosen(((i >> 1) == j) & (i < nz))
    return rows, lanes


def pool(value, matrices):
    planes = value.shape[0]
    flat = value.reshape(planes * 8, 128)
    small = times_left(matrices[0], times_right(flat, matrices[1]))
    return small.reshape(planes // 2, 8, 128)


def coarse_index(index, level, dim, length, coarse_length):
    off = ring_offset(index, SIZE[level][dim], length) >> 1
    return jnp.where(off < 0, off + coarse_length, off)


def spread_matrices(level):
    shape = (PLANES[level] * ROWS, PLANES[level + 1] * ROWS)
    i, j = iota(shape, 0), iota(shape, 1)
    x_match = coarse_index(i >> 4, level, 0, PLANES[level], PLANES[level + 1]) == (j >> 4)
    y_match = coarse_index(i & 15, level, 1, ROWS, ROWS) == (j & 15)
    rows = as_chosen(x_match & y_match)
    shape = (128, LANES[level])
    i, j = iota(shape, 0), iota(shape, 1)
    lanes = as_chosen(coarse_index(j, level, 2, LANES[level], 128) == i)
    return rows, lanes


def spread(value, matrices, level):
    flat = value.reshape(PLANES[level + 1] * ROWS, 128)
    wide = times_left(matrices[0], times_right(flat, matrices[1]))
    return wide.reshape(PLANES[level], ROWS, LANES[level])


def all_peers():
    steps = neighbours(2)
    steps += [(0, step, 0) for step in range(1, 16)]
    steps += [(step // 8, 0, step % 8) for step in range(1, 32)]
    return {tuple(step % COUNT[axis] for axis, step in zip(AXES, triple)) for triple in steps}


def kernel(f_ref, k_ref, m_ref, agg_ref, inverse_ref, out_ref, *scratch):
    n_ex = len(EXCHANGES) * PER_EXCHANGE
    ex_bufs = [scratch[PER_EXCHANGE * e : PER_EXCHANGE * (e + 1)] for e in range(len(EXCHANGES))]
    co_bufs = [scratch[n_ex + PER_COARSE * c : n_ex + PER_COARSE * (c + 1)] for c in range(CYCLES)]
    keep = scratch[n_ex + PER_COARSE * CYCLES :]
    coef = keep[0:15]
    onehot_lo, onehot_hi, state0, state1 = keep[15:19]
    source = keep[19:22]
    spread_rows, spread_lanes = keep[22:24], keep[24:26]

    barrier = pltpu.get_barrier_semaphore()
    greeted = sorted(all_peers())
    for steps in greeted:
        target = {axis: peer(axis, step) for axis, step in zip(AXES, steps) if step != 0}
        pl.semaphore_signal(barrier, inc=1, device_id=target, device_id_type=MESH)

    pools = [pool_matrices(0), pool_matrices(1)]
    ks, ms = [k_ref[...]], [m_ref[...]]
    for level in range(2):
        ks.append(pool(ks[level], pools[level]) * 0.125)
        ms.append(pool(ms[level], pools[level]))
    pl.semaphore_wait(barrier, len(greeted))

    def meanwhile():
        for level in range(2):
            spread_rows[level][...], spread_lanes[level][...] = spread_matrices(level)
        lanes_of = iota((128, 128), 0)
        highs = iota((16, 128), 0)
        for i in range(8):
            row = agg_ref[i : i + 1, :]
            onehot_lo[:, 128 * i : 128 * i + 128] = as_chosen(((row & 127) == lanes_of) & (row >= 0))
            onehot_hi[:, 128 * i : 128 * i + 128] = jnp.where((row >> 7) == highs, 1.0, 0.0)

    used = iter(ex_bufs)
    rings = exchange(
        [
            (0, next(used), [ks[0], ms[0], f_ref[...]]),
            (1, next(used), [ks[1], ms[1]]),
            (2, next(used), [ks[2], ms[2]]),
        ],
        meanwhile,
    )
    for level in range(3):
        kp_ref, sk_ref, d_ref, g_ref, in_ref = coef[5 * level : 5 * level + 5]
        ok = inside(level)
        kp = jnp.where(ok, rings[level][0], 1.0)
        scaled = 2.0**level * kp
        diagonal = scaled * smooth_sum(kp) + rings[level][1]
        kp_ref[...] = kp
        sk_ref[...] = scaled
        d_ref[...] = diagonal
        g_ref[...] = jnp.where(ok, OMEGA / diagonal, 0.0)
        in_ref[...] = jnp.where(ok, 1.0, 0.0)
    source[0][...] = rings[0][2]

    def residual(level, value):
        kp_ref, sk_ref, d_ref, _, _ = coef[5 * level : 5 * level + 5]
        around = smooth_sum(kp_ref[...] * value)
        return source[level][...] - d_ref[...] * value + sk_ref[...] * around

    def sweep(level, value):
        return value + coef[5 * level + 3][...] * residual(level, value)

    def start(level):
        return coef[5 * level + 3][...] * source[level][...]

    def swap(level, block):
        return exchange([(level, next(used), [block])])[0][0]

    def aggregate_fix(rest, bufs):
        mine, from_gy, at_gy, from_xz, partial, pieces, ss, rs = bufs
        rows = [rest[i // 2, i % 2 : i % 2 + 1, :] for i in range(8)]
        left = jnp.concatenate([onehot_hi[:, 128 * i : 128 * i + 128] * rows[i] for i in range(8)], axis=1)
        sums = sum(
            lax.dot_general(piece, onehot_lo[...], (((1,), (1,)), ((), ())), preferred_element_type=F32)
            for piece in parts(left)
        )
        for j in range(16):
            mine[j] = sums[j : j + 1, :]
        copies = []
        for step in range(1, 16):
            copies.append(send(mine.at[peer("gy", step)], from_gy.at[step], ss.at[step], rs.at[step], "gy", step))
        for copy in copies:
            copy.wait()
        total = mine[lax.axis_index("gy")]
        for step in range(1, 16):
            total = total + from_gy[step]
        at_gy[...] = total
        copies = []
        for step in range(1, 32):
            steps = (step // 8, 0, step % 8)
            copies.append(send_to(at_gy, from_xz.at[step], ss.at[15 + step], rs.at[15 + step], steps))
        for copy in copies:
            copy.wait()
        for step in range(1, 32):
            total = total + from_xz[step]
        down = jnp.broadcast_to(total, (128, 128)).T
        for j in range(16):
            product = down * inverse_ref[:, 128 * j : 128 * j + 128]
            partial[j : j + 1, :] = jnp.sum(product, axis=0, keepdims=True)
        copies = []
        for step in range(1, 16):
            at = 46 + step
            copies.append(send(partial, pieces.at[step], ss.at[at], rs.at[at], "gy", step))
        for copy in copies:
            copy.wait()
        fixes = partial[...]
        for step in range(1, 16):
            fixes = fixes + pieces[step]
        wide = times_right(fixes, onehot_lo[...])
        cells = jnp.sum(wide * onehot_hi[...], axis=0, keepdims=True)
        row = iota((8, 128), 0)
        planes = []
        for x in range(4):
            even = cells[:, 256 * x : 256 * x + 128]
            odd = cells[:, 256 * x + 128 : 256 * x + 256]
            planes.append(jnp.where(row == 0, even, jnp.where(row == 1, odd, 0.0)))
        return jnp.stack(planes, axis=0)

    value = start(0)
    for turn in range(CYCLES):
        if turn > 0:
            value = sweep(0, value)
        value = sweep(0, value)
        rest = residual(0, value)[0:16, 0:8, 0:128]
        state0[...] = value
        source[1][...] = swap(1, pool(rest, pools[0]))
        value = sweep(1, start(1))
        rest = residual(1, value)[0:8, 0:8, :]
        state1[...] = value
        source[2][...] = swap(2, pool(rest, pools[1]))
        value = sweep(2, start(2))
        rest = residual(2, value)[0:4, 0:8, :]
        fixed = value[0:4, 0:8, :] + aggregate_fix(rest, co_bufs[turn])
        value = swap(2, fixed) * coef[14][...]
        value = sweep(2, sweep(2, value))
        value = state1[...] + spread(value, (spread_rows[1][...], spread_lanes[1][...]), 1)
        value = sweep(1, sweep(1, value))
        value = swap(1, value[0:8, 0:8, :]) * coef[9][...]
        value = state0[...] + spread(value, (spread_rows[0][...], spread_lanes[0][...]), 0)
        value = sweep(0, sweep(0, value))
        if turn + 1 < CYCLES:
            value = swap(0, value[0:16, 0:8, 0:128]) * coef[4][...]
    out_ref[...] = value[0:16, 0:8, 0:128]


def local(right_side, conduct, mass, aggregate_of, coarse_inverse):
    agg = jnp.pad(aggregate_of.reshape(8, 32), ((0, 0), (0, 96)), constant_values=-1)
    scratch = []
    for level, fields in EXCHANGES:
        scratch += exchange_scratch(level, fields)
    for _ in range(CYCLES):
        scratch += coarse_scratch()
    rings = [pltpu.VMEM((PLANES[level], ROWS, LANES[level]), F32) for level in range(3)]
    for ring in rings:
        scratch += [ring] * 5
    scratch += [pltpu.VMEM((128, 1024), BF16), pltpu.VMEM((16, 1024), F32), rings[0], rings[1]]
    scratch += rings
    scratch += [pltpu.VMEM((PLANES[level] * ROWS, PLANES[level + 1] * ROWS), BF16) for level in range(2)]
    scratch += [pltpu.VMEM((128, LANES[level]), BF16) for level in range(2)]
    return pl.pallas_call(
        kernel,
        out_shape=jax.ShapeDtypeStruct(right_side.shape, F32),
        in_specs=[pl.BlockSpec(memory_space=pltpu.VMEM)] * 5,
        out_specs=pl.BlockSpec(memory_space=pltpu.VMEM),
        scratch_shapes=scratch,
        compiler_params=pltpu.CompilerParams(collective_id=0, has_side_effects=True),
    )(right_side, conduct, mass, agg, coarse_inverse)


def solution(mesh):
    return jax.shard_map(
        local,
        mesh=mesh,
        in_specs=(
            P("gx", "gy", "gz"),
            P("gx", "gy", "gz"),
            P("gx", "gy", "gz"),
            P("gx", "gy", "gz"),
            P("gy", None),
        ),
        out_specs=P("gx", "gy", "gz"),
        check_vma=False,
    )
```
